32 devices in a mesh: dp: 8 (over y, x, core), tensor: 4 (over z).
Axes of the slice: x: 2, y: 2, z: 4, core: 2. Of those that a mesh axis runs over, the one named last changes fastest.
Arguments:
- prefill_states: bfloat16 [64, 2, 64, 128, 128], P('dp', None, 'tensor'), may hold values from -6 to 6
- prompt_slot: int32 [64], replicated, may hold values from 0 to 63, as said below
- sample_prompt: int32 [1024], P('dp'), may hold values from 0 to 63, as said below
- queries: bfloat16 [1024, 2, 2, 8192], P('dp', None, None, 'tensor'), may hold values from -2 to 2
- keys: bfloat16 [1024, 2, 2, 8192], P('dp', None, None, 'tensor'), may hold values from -3 to 3
- values: bfloat16 [1024, 2, 2, 8192], P('dp', None, None, 'tensor'), may hold values from -6 to 6
- gates: bfloat16 [1024, 2, 2, 8192], P('dp', None, None, 'tensor'), may hold values from -6 to 6
- norm_gain: float32 [2, 8192], P(None, 'tensor'), may hold values from 0.25 to 1.75
- decay_rate: float32 [2, 64], P(None, 'tensor'), may hold values from 0.01 to 1
Outputs:
- attended: float32 [1024, 2, 2, 8192], P('dp', None, None, 'tensor')
The draws below stay inside these ranges and needn't reach their ends.
Inputs may be any that keep to these rules, and one draw needn't show every extreme that they name: `prompt_slot`: A permutation: each slot holds one prompt; slot s lies with dp group s // 8. `sample_prompt`: rows g * 128 to (g + 1) * 128 - 1 hold, for r = 0 to 3, exactly 4 rows of each prompt whose slot lies with group (g - r * 2) modulo 64 / 8, in any order.
All inputs are finite; a program needn't handle non-finite values.
Results may differ from the reference program's by a relative error of at most 0.0003.
Values may be sent and summed in bfloat16 or wider, within the bound.
No kernel may reach another device: no remote copies, remote signals or barrier semaphores. Data moves between devices by JAX's collectives and lax.ppermute only.
A program may use at most 64 MiB of HBM per device.

```python
import math
import jax
import jax.numpy as jnp
from jax import lax

HEADS = 64
HEAD_DIM = 128
LAYERS = 2
STEPS = 2
READERS = 4
SAMPLES_PER = 16
PR_DEV = 8
PROMPTS = 64
SAMPLES = 1024
QUARTER = 2


def slot_order(key):
    return jax.random.permutation(jax.random.fold_in(key, 101), PROMPTS).astype(jnp.int32)


def draw_prompt_slot(key, part):
    return slot_order(key)


def draw_sample_prompt(key, part):
    order = slot_order(key)
    prompt_at = jnp.zeros((PROMPTS,), jnp.int32).at[order].set(jnp.arange(PROMPTS, dtype=jnp.int32))
    groups = PROMPTS // PR_DEV
    reach = jnp.arange(READERS, dtype=jnp.int32)
    within = jnp.arange(PR_DEV, dtype=jnp.int32)
    copies = SAMPLES_PER // READERS
    shuffle_key = jax.random.fold_in(key, 202)

    def one_group(group):
        source = (group - reach * QUARTER) % groups
        slots = (source[:, None] * PR_DEV + within[None, :]).reshape(-1)
        slots = jnp.repeat(slots, copies)
        shuffled = jax.random.permutation(jax.random.fold_in(shuffle_key, group), slots)
        return prompt_at[shuffled]
    return jax.vmap(one_group)(jnp.arange(groups, dtype=jnp.int32)).reshape(-1).astype(jnp.int32)


def draw_queries(key, part):
    columns = HEADS * HEAD_DIM
    head = jnp.arange(columns) // HEAD_DIM
    rise = 3.0 ** (0.5 * head.astype(jnp.float32) / max(HEADS - 1, 1))
    head_factor = jnp.exp(jax.random.uniform(jax.random.fold_in(key, 7), (HEADS,), minval=0.0, maxval=math.log(3.2)))[head]
    shape = (SAMPLES, STEPS, LAYERS, columns)
    row_factor = jnp.exp(jax.random.uniform(jax.random.fold_in(key, 8), (SAMPLES, 1, 1, 1), minval=0.0, maxval=math.log(3.2)))
    base = jax.random.normal(jax.random.fold_in(key, 9), shape)
    drawn = base * HEAD_DIM ** (-0.5) * rise * head_factor * row_factor
    return jnp.clip(drawn, -2.0, 2.0).astype(jnp.bfloat16)


def steps_of(rng, dims, split, low, high):
    factor_of, own = 1.0, jax.random.fold_in(rng, 6)
    for axis_at, shards_of in split:
        heights = jnp.exp(jax.random.uniform(jax.random.fold_in(own, axis_at), (shards_of,), jnp.float32, low / len(split), high / len(split)))
        factor_of = factor_of * jnp.repeat(heights, dims[axis_at] // shards_of).reshape([-1 if axis == axis_at else 1 for axis in range(len(dims))])
    return factor_of


def bell_draw(key, extent, spread, bound, cuts=(), kind=jnp.bfloat16):
    values = spread * jax.random.normal(key, extent, jnp.float32)
    if cuts:
        values = values * steps_of(key, extent, cuts, -0.22, 0.18)
    return jnp.clip(values, -bound, bound).astype(kind)


def setup_inputs(seed: int = 0) -> dict:
    seeds = jax.random.split(jax.random.key(seed), 10)
    prefill_states = bell_draw(seeds[0], (PROMPTS, LAYERS, HEADS, HEAD_DIM, HEAD_DIM), 1.0, 6.0, ((0, 8), (2, 4)))
    prompt_slot = draw_prompt_slot(jax.random.fold_in(seeds[9], 71), 0)
    sample_prompt = draw_sample_prompt(jax.random.fold_in(seeds[9], 71), 0)
    queries = draw_queries(jax.random.fold_in(seeds[9], 71), 0)
    keys = bell_draw(seeds[4], (SAMPLES, STEPS, LAYERS, HEADS * HEAD_DIM), 0.5, 3.0, ((0, 8), (3, 4)))
    values = bell_draw(seeds[5], (SAMPLES, STEPS, LAYERS, HEADS * HEAD_DIM), 1.0, 6.0, ((0, 8), (3, 4)))
    gates = bell_draw(seeds[6], (SAMPLES, STEPS, LAYERS, HEADS * HEAD_DIM), 1.0, 6.0, ((0, 8), (3, 4)))
    norm_gain = jnp.clip(1.0 + 0.15 * jax.random.normal(seeds[7], (LAYERS, HEADS * HEAD_DIM), jnp.float32), 0.25, 1.75)
    decay_rate = jnp.clip(jnp.exp(math.log(1.0) - 4.6051702 * jax.random.uniform(seeds[8], (LAYERS, HEADS), jnp.float32) ** steps_of(seeds[8], (LAYERS, HEADS), ((1, 4),), -0.2, 0.2)), 0.01, 1.0)
    return dict(prefill_states=prefill_states, prompt_slot=prompt_slot, sample_prompt=sample_prompt, queries=queries, keys=keys, values=values, gates=gates, norm_gain=norm_gain, decay_rate=decay_rate)


def reference(prefill_states, prompt_slot, sample_prompt, queries, keys, values, gates, norm_gain, decay_rate):
    retain = jnp.exp(-decay_rate)[None, :, :, None]
    shape = (SAMPLES, STEPS, LAYERS, HEADS, HEAD_DIM)
    query_all = queries.astype(jnp.float32).reshape(shape)
    key_all = keys.astype(jnp.float32).reshape(shape)
    value_all = values.astype(jnp.float32).reshape(shape)
    slots = prompt_slot[sample_prompt].astype(jnp.int32)

    def one_row(pair):
        slot, query_row = pair
        state = prefill_states[slot].astype(jnp.float32)
        return jnp.einsum('jlhd,lhde->jlhe', query_row, state, precision=lax.Precision.HIGHEST)
    reach = lax.map(one_row, (slots, query_all))
    first_first = lax.optimization_barrier(jnp.sum(query_all[:, 0] * key_all[:, 0], axis=-1))[..., None]
    second_first = lax.optimization_barrier(jnp.sum(query_all[:, 1] * key_all[:, 0], axis=-1))[..., None]
    second_second = lax.optimization_barrier(jnp.sum(query_all[:, 1] * key_all[:, 1], axis=-1))[..., None]
    out_one = retain * reach[:, 0] + first_first * value_all[:, 0]
    out_two = retain * retain * reach[:, 1] + retain * second_first * value_all[:, 0] + second_second * value_all[:, 1]
    mixed = jnp.stack([out_one, out_two], axis=1).reshape(SAMPLES, STEPS, LAYERS, HEADS * HEAD_DIM)
    total = lax.optimization_barrier(jnp.sum(mixed * mixed, axis=-1))
    scale = lax.rsqrt(total / (HEADS * HEAD_DIM) + 1e-05)
    return mixed * scale[..., None] * norm_gain[None, None] * jax.nn.sigmoid(gates.astype(jnp.float32))
```

```python
import functools

import jax
import jax.numpy as jnp
from jax import lax
from jax.experimental import pallas as pl
from jax.experimental.pallas import tpu as pltpu
from jax.sharding import PartitionSpec as P

HEADS = 64
HEAD_DIM = 128
LANES = 128
ANY = pl.BlockSpec(memory_space=pl.ANY)
SMEM = pl.BlockSpec(memory_space=pltpu.SMEM)
VMEM = pl.BlockSpec(memory_space=pltpu.VMEM)
TOP = 32767.0
ROUND = 12582912.0


def params(mib):
    return pltpu.CompilerParams(vmem_limit_bytes=mib << 20)


def cost(flops, moved):
    return pl.CostEstimate(flops=flops, bytes_accessed=moved, transcendentals=0)


def rows_view(x):
    rows, steps, layers, columns = x.shape
    heads = columns // LANES
    x = x.reshape(rows, steps, layers, heads, LANES).transpose(0, 1, 3, 2, 4)
    return x.reshape(rows, steps * heads * layers, LANES)


def rows_unview(y, steps, layers):
    rows, lines, _ = y.shape
    heads = lines // (steps * layers)
    y = y.reshape(rows, steps, heads, layers, LANES).transpose(0, 1, 3, 2, 4)
    return y.reshape(rows, steps, layers, heads * LANES)


def iota(shape, axis):
    return lax.broadcasted_iota(jnp.int32, shape, axis)


def pack_rows(order_ref, first, prompts, q_ref, scratch, out_ref):
    lines = q_ref.shape[1]
    half = lines // 2
    total = out_ref.shape[1]
    samples = total // lines

    def body(p, carry):
        for c in range(samples):
            s = order_ref[0, first + p * samples + c]
            for j in range(2):
                block = q_ref[s, j * half : (j + 1) * half, :].astype(jnp.float32)
                scratch[p % 2, pl.ds(c * 2 + j, half, stride=2 * samples), :] = block
        out_ref[p] = scratch[p % 2].astype(jnp.bfloat16)
        return carry

    lax.fori_loop(0, prompts, body, 0, unroll=2)


def order_kernel(
    owned, quarter, chunks, place_ref, slot_ref, prompt_ref, q_hbm,
    order_ref, *rest,
):
    outs, (q_vmem, line, scratch, sems) = rest[: len(chunks)], rest[len(chunks) :]
    load = pltpu.make_async_copy(q_hbm, q_vmem, sems.at[0])
    load.start()
    rows = prompt_ref.shape[1]
    count = slot_ref.shape[1]
    per = rows // (4 * owned)
    f32 = jnp.float32
    slot = slot_ref[...]
    owner = lax.div(lax.div(slot, owned), quarter)
    table = ((owner ^ place_ref[0, 0]) * owned + lax.rem(slot, owned)).astype(f32)
    down, across = iota((rows, rows), 0), iota((rows, rows), 1)
    prompt = jnp.broadcast_to(prompt_ref[...].astype(f32), (rows, rows))
    prompt = jnp.sum(jnp.where(down == across, prompt, 0.0), axis=1, keepdims=True)
    hit = prompt == iota((rows, count), 1).astype(f32)
    key = jnp.sum(jnp.where(hit, jnp.broadcast_to(table, (rows, count)), 0.0), axis=1, keepdims=True)
    key_all = jnp.broadcast_to(key, (rows, rows))
    key_row = jnp.sum(jnp.where(down == across, key_all, 0.0), axis=0, keepdims=True)
    same = (key_all == jnp.broadcast_to(key_row, (rows, rows))) & (across < down)
    rank = jnp.sum(jnp.where(same, 1.0, 0.0), axis=1, keepdims=True)
    spot = key * per + rank
    found = jnp.broadcast_to(spot, (rows, rows)) == across.astype(f32)
    line[...] = jnp.sum(jnp.where(found, down.astype(f32), 0.0), axis=0, keepdims=True).astype(jnp.int32)
    note = pltpu.make_async_copy(line, order_ref, sems.at[1])
    note.start()
    note.wait()
    load.wait()
    for chunk, out_ref in zip(chunks, outs):
        pack_rows(order_ref, chunk * owned * per, owned, q_vmem, scratch, out_ref)


def pack_kernel(owned, per, chunks, order_ref, q_ref, *rest):
    outs, scratch = rest[:-1], rest[-1]
    for chunk, out_ref in zip(chunks, outs):
        pack_rows(order_ref, chunk * owned * per, owned, q_ref, scratch, out_ref)


def reach_kernel(coded, q_ref, s_ref, out_ref, *scratch):
    heads = s_ref.shape[2]
    lines = q_ref.shape[1]
    p = pl.program_id(0)
    first = p * lines if coded else 0

    def products(h):
        a = q_ref[0, h * 16 : (h + 1) * 16, :]
        w = jnp.concatenate([s_ref[0, 0, h], s_ref[0, 1, h]], axis=1)
        y = jnp.dot(a, w, preferred_element_type=jnp.float32)
        return y[:8, :LANES], y[8:, LANES:]

    if not coded:
        for h in range(heads):
            for l, r in enumerate(products(h)):
                at = h * 16 + l * 8
                out_ref[0, at : at + 8, :] = r
        return
    exact, power = scratch
    lane = iota((8, LANES), 1)
    base = (p // 2) * 2 * heads
    peak = jnp.ones((8, LANES), jnp.float32)
    for h in range(heads):
        for l, r in enumerate(products(h)):
            at = h * 16 + l * 8
            exact[at : at + 8, :] = r
            top = jnp.max(jnp.abs(r), axis=1, keepdims=True)
            peak = jnp.where(lane == h * 2 + l, top, peak)
    e = jnp.ceil(jnp.log2(jnp.maximum(peak, 1e-32)) + 1e-4)
    factor = jnp.exp2(15.0 - e) * (TOP / 32768.0)
    row = pl.multiple_of((p % 2) * 8, 8)
    mine = (lane >= base) & (lane < base + 2 * heads)
    spread = jnp.concatenate([e[:, : 2 * heads]] * (LANES // (2 * heads)), axis=1)
    power[pl.ds(row, 8), :] = jnp.where(mine, spread, power[pl.ds(row, 8), :])
    for h in range(heads):
        code = []
        for l in range(2):
            at = h * 16 + l * 8
            f = jnp.broadcast_to(factor[:, h * 2 + l : h * 2 + l + 1], (8, LANES))
            code.append((exact[at : at + 8, :] * f + ROUND) - ROUND)
        code = jnp.concatenate(code, axis=0).astype(jnp.int32).astype(jnp.int16)
        out_ref[pl.ds(pl.multiple_of(first + h * 16, 16), 16), :] = code

    @pl.when(p == pl.num_programs(0) - 1)
    def _():
        tail = pl.num_programs(0) * lines
        out_ref[pl.ds(pl.multiple_of(tail, 16), 16), :] = power[...].astype(jnp.int32).astype(jnp.int16)


def reach(query, states, first, prompts, coded):
    _, lines, _ = query.shape
    _, layers, heads, _, _ = states.shape
    if coded:
        shape = jax.ShapeDtypeStruct((prompts * lines + 16, LANES), jnp.int16)
        scratch = [pltpu.VMEM((lines, LANES), jnp.float32), pltpu.VMEM((16, LANES), jnp.float32)]
        out = pl.BlockSpec(shape.shape, lambda p: (0, 0))
    else:
        shape = jax.ShapeDtypeStruct((prompts, lines, LANES), jnp.float32)
        out = pl.BlockSpec((1, lines, LANES), lambda p: (p, 0, 0))
        scratch = []
    return pl.pallas_call(
        functools.partial(reach_kernel, coded),
        grid=(prompts,),
        in_specs=[
            pl.BlockSpec((1, lines, LANES), lambda p: (first + p, 0, 0)),
            pl.BlockSpec((1, layers, heads, LANES, LANES), lambda p: (first + p, 0, 0, 0, 0)),
        ],
        out_specs=out,
        out_shape=shape,
        scratch_shapes=scratch,
        compiler_params=params(24),
        cost_estimate=cost(prompts * lines * LANES * LANES * 4, prompts * layers * heads * LANES * LANES * 2),
        name="reach",
    )(query, states)


def prepare_kernel(block, order_ref, q_ref, k_ref, v_ref, g_ref, retain_ref, gain_ref, own_ref, gate_ref):
    half = q_ref.shape[1] // 2
    first = pl.program_id(0) * block
    retain, gain = retain_ref[...], gain_ref[...]
    f32 = jnp.float32

    def body(i, carry):
        s = order_ref[0, first + i]
        one, two = slice(0, half), slice(half, 2 * half)
        q1, q2 = q_ref[s, one, :].astype(f32), q_ref[s, two, :].astype(f32)
        k1, k2 = k_ref[s, one, :].astype(f32), k_ref[s, two, :].astype(f32)
        v1, v2 = v_ref[s, one, :].astype(f32), v_ref[s, two, :].astype(f32)
        first_first = jnp.sum(q1 * k1, axis=1, keepdims=True)
        second_first = jnp.sum(q2 * k1, axis=1, keepdims=True)
        second_second = jnp.sum(q2 * k2, axis=1, keepdims=True)
        own_ref[i, one, :] = first_first * v1
        own_ref[i, two, :] = retain * second_first * v1 + second_second * v2
        gate_ref[i, one, :] = gain * jax.nn.sigmoid(g_ref[s, one, :].astype(f32))
        gate_ref[i, two, :] = gain * jax.nn.sigmoid(g_ref[s, two, :].astype(f32))
        return carry

    lax.fori_loop(0, block, body, 0, unroll=2)


def combine_kernel(coded, first, *refs):
    if coded:
        code_ref, power_ref, own_ref, gate_ref, retain_ref, sum_in, out_ref, sum_ref, exact = refs
    else:
        code_ref, own_ref, gate_ref, retain_ref, sum_in, out_ref, sum_ref = refs
    samples, lines, _ = own_ref.shape
    half = lines // 2
    p = pl.program_id(0)
    lane = iota((8, LANES), 1)
    if coded:
        row = pl.multiple_of((p % 2) * 8, 8)
        power = power_ref[...].astype(jnp.int32).astype(jnp.float32)
        power = jnp.where(p % 2 == 0, power[:8], power[8:])
        unit = jnp.exp2(power - 15.0) * (32768.0 / TOP)
        unit = pltpu.roll(unit, lax.rem(LANES - (p // 2) * half, LANES), 1)
        for h in range(half // 2):
            code = code_ref[h * 16 : (h + 1) * 16, :].astype(jnp.int32).astype(jnp.float32)
            for l in range(2):
                at = h * 16 + l * 8
                u = jnp.broadcast_to(unit[:, h * 2 + l : h * 2 + l + 1], (8, LANES))
                exact[at : at + 8, :] = code[l * 8 : l * 8 + 8] * u
        reached = exact
    else:
        reached = code_ref.at[0]

    @pl.when(p == 0)
    def _():
        sum_ref[...] = jnp.zeros_like(sum_ref)

    retain = retain_ref[...]
    squared = retain * retain
    totals = [sum_ref[:8], sum_ref[8:]]
    for c in range(samples):
        for j in range(2):
            at = slice(j * half, (j + 1) * half)
            r = reached[pl.ds(c * 2 + j, half, stride=2 * samples), :]
            mixed = (squared if j else retain) * r + own_ref[c, at, :]
            out_ref[c, at, :] = mixed * gate_ref[c, at, :]
            power = jnp.sum((mixed * mixed).reshape(half // 8, 8, LANES), axis=0)
            power = jnp.sum(power, axis=1, keepdims=True)
            totals[j] = jnp.where(lane == first + p * samples + c, power, totals[j])
    sum_ref[:8] = totals[0]
    sum_ref[8:] = totals[1]

    @pl.when(p == pl.num_programs(0) - 1)
    def _():
        for j in range(2):
            t = sum_ref[j * 8 : j * 8 + 8]
            u = t + pltpu.roll(t, 4, 0)
            sum_ref[j * 8 : j * 8 + 8] = u + pltpu.roll(u, 2, 0) + sum_in[j * 8 : j * 8 + 8]


def combine(coded, products, own, gate, retain, sums, start, prompts, first):
    lines = own.shape[1]
    total = products.shape[1] if not coded else (products.shape[0] - 16) // prompts
    samples = total // lines
    specs = [
        pl.BlockSpec((samples, lines, LANES), lambda p: (start + p, 0, 0)),
        pl.BlockSpec((samples, lines, LANES), lambda p: (start + p, 0, 0)),
        pl.BlockSpec(retain.shape, lambda p: (0, 0)),
        pl.BlockSpec((16, LANES), lambda p: (0, 0)),
    ]
    if coded:
        end = prompts * total // 16
        lead = [
            pl.BlockSpec((total, LANES), lambda p: (p, 0)),
            pl.BlockSpec((16, LANES), lambda p: (end, 0)),
        ]
        given = [products, products]
        scratch = [pltpu.VMEM((total, LANES), jnp.float32)]
    else:
        lead = [pl.BlockSpec((1, total, LANES), lambda p: (p, 0, 0))]
        given = [products]
        scratch = []
    return pl.pallas_call(
        functools.partial(combine_kernel, coded, first),
        grid=(prompts,),
        in_specs=lead + specs,
        out_specs=[
            pl.BlockSpec((samples, lines, LANES), lambda p: (p, 0, 0)),
            pl.BlockSpec((16, LANES), lambda p: (0, 0)),
        ],
        out_shape=[
            jax.ShapeDtypeStruct((prompts * samples, lines, LANES), jnp.float32),
            jax.ShapeDtypeStruct((16, LANES), jnp.float32),
        ],
        scratch_shapes=scratch,
        compiler_params=params(16),
        cost_estimate=cost(0, prompts * samples * lines * LANES * 14),
        name="combine",
    )(*given, own, gate, retain, sums)


def finish_kernel(features, first, splits, count, aliased, order_ref, *refs):
    tiles, refs = refs[:count], refs[count:]
    parts, refs = refs[: len(splits)], refs[len(splits) :]
    if aliased:
        refs = refs[1:]
    out_hbm, scratch, scale, sem = refs
    lines = parts[0].shape[1]
    half = lines // 2
    total = sum(t[...] for t in tiles)
    scale[...] = lax.rsqrt(total / features + 1e-05)
    lane = iota((8, LANES), 1)
    at = 0
    for part, count in zip(parts, splits):

        def body(i, carry, part=part, at=at):
            row = at + i
            for j in range(2):
                one = jnp.where(lane == row, scale[j * 8 : j * 8 + 8, :], 0.0)
                one = jnp.sum(one, axis=1, keepdims=True)
                block = part[i, j * half : (j + 1) * half, :].reshape(half // 8, 8, LANES)
                scratch[row, j * half : (j + 1) * half, :] = (block * one[None]).reshape(half, LANES)
            s = order_ref[0, first + row]
            pltpu.make_async_copy(scratch.at[row], out_hbm.at[s], sem).start()
            return carry

        lax.fori_loop(0, count, body, 0, unroll=2)
        at += count
    rows = scratch.shape[0]
    pltpu.make_async_copy(scratch, out_hbm.at[pl.ds(0, rows)], sem).wait()


def finish(order, tiles, parts, first, out, rows):
    splits = tuple(p.shape[0] for p in parts)
    lines = parts[0].shape[1]
    given = [order, *tiles, *parts] + ([out] if out is not None else [])
    specs = [SMEM] + [VMEM] * (len(tiles) + len(parts)) + ([ANY] if out is not None else [])
    count = sum(splits)
    return pl.pallas_call(
        functools.partial(finish_kernel, HEADS * HEAD_DIM, first, splits, len(tiles), out is not None),
        in_specs=specs,
        out_specs=ANY,
        out_shape=jax.ShapeDtypeStruct((rows, lines, LANES), jnp.float32),
        scratch_shapes=[
            pltpu.VMEM((count, lines, LANES), jnp.float32),
            pltpu.VMEM((16, LANES), jnp.float32),
            pltpu.SemaphoreType.DMA,
        ],
        input_output_aliases={len(given) - 1: 0} if out is not None else {},
        compiler_params=params(16),
        cost_estimate=cost(0, count * lines * LANES * 8),
        name="finish",
    )(*given)


def local(
    prefill_states, prompt_slot, sample_prompt, queries, keys, values, gates, norm_gain, decay_rate
):
    group = lax.axis_index("dp")
    groups = lax.axis_size("dp")
    split = lax.axis_size("tensor")
    quarter = groups // 4
    owned = prefill_states.shape[0]
    rows, steps, layers, columns = queries.shape
    heads = columns // LANES
    per = rows // (4 * owned)
    lines = steps * layers * heads
    assert steps == 2 and layers == 2 and per * steps == 8 and rows <= LANES
    assert heads % 4 == 0 and heads * layers * owned <= 2 * LANES

    def swap(block, bits):
        far = [((i // quarter) ^ bits) * quarter + i % quarter for i in range(groups)]
        return lax.ppermute(block, "dp", [(f, i) for i, f in enumerate(far)])

    def shared(tile):
        if split > 4:
            return [lax.psum(tile, "tensor")]
        return [tile] + [
            lax.ppermute(tile, "tensor", [(i, (i + k) % split) for i in range(split)])
            for k in range(1, split)
        ]

    q, k, v, g = (rows_view(x) for x in (queries, keys, values, gates))
    gain = rows_view(norm_gain[None, None]).reshape(heads * layers, LANES)
    retain = jnp.exp(-decay_rate).T.reshape(heads * layers, 1)
    retain = jnp.broadcast_to(retain, (heads * layers, LANES))
    place = (group // quarter).astype(jnp.int32).reshape(1, 1)

    packed = jax.ShapeDtypeStruct((owned, per * lines, LANES), jnp.bfloat16)
    pack_scratch = pltpu.VMEM((2, per * lines, LANES), jnp.float32)
    order, near, next_ = pl.pallas_call(
        functools.partial(order_kernel, owned, quarter, (1, 2)),
        in_specs=[SMEM, VMEM, VMEM, ANY],
        out_specs=[SMEM, VMEM, VMEM],
        out_shape=[jax.ShapeDtypeStruct((1, rows), jnp.int32), packed, packed],
        scratch_shapes=[
            pltpu.VMEM(q.shape, q.dtype),
            pltpu.VMEM((1, rows), jnp.int32),
            pack_scratch,
            pltpu.SemaphoreType.DMA((2,)),
        ],
        compiler_params=params(16),
        cost_estimate=cost(0, 4 << 20),
        name="order",
    )(place, prompt_slot.reshape(1, -1), sample_prompt.reshape(1, -1), q)
    near, next_ = swap(near, 1), swap(next_, 2)
    far, mine = pl.pallas_call(
        functools.partial(pack_kernel, owned, per, (3, 0)),
        in_specs=[SMEM, VMEM],
        out_specs=[VMEM, VMEM],
        out_shape=[packed, packed],
        scratch_shapes=[pack_scratch],
        compiler_params=params(16),
        cost_estimate=cost(0, 4 << 20),
        name="pack",
    )(order, q)
    order, far, mine = lax.optimization_barrier((order, far, mine))
    far = swap(far, 3)

    block = rows // 8
    whole = pl.BlockSpec(q.shape, lambda i: (0, 0, 0))
    flat = pl.BlockSpec(retain.shape, lambda i: (0, 0))
    piece = pl.BlockSpec((block, lines, LANES), lambda i: (i, 0, 0))
    own, gate = pl.pallas_call(
        functools.partial(prepare_kernel, block),
        grid=(rows // block,),
        in_specs=[SMEM] + [whole] * 4 + [flat] * 2,
        out_specs=[piece, piece],
        out_shape=[jax.ShapeDtypeStruct(q.shape, jnp.float32)] * 2,
        compiler_params=params(32),
        cost_estimate=cost(0, 16 << 20),
        name="prepare",
    )(order, q, k, v, g, retain, gain)

    def after(value, *done):
        return lax.optimization_barrier((value, *done))[0]

    zero = jnp.zeros((16, LANES), jnp.float32)
    mine = reach(mine, prefill_states, 0, owned, False)
    near_code = reach(after(near, mine, own), prefill_states, 0, owned, True)
    near = swap(near_code, 1)
    next_code = reach(after(next_, near_code), prefill_states, 0, owned, True)
    next_ = swap(next_code, 2)
    part = owned // 2
    far = after(far, next_code)
    low_code = reach(far, prefill_states, 0, part, True)
    far_low = swap(low_code, 3)
    high_code = reach(after(far, low_code), prefill_states, part, part, True)
    far_high = swap(high_code, 3)

    chunk = owned * per
    out0, sums = combine(False, after(mine, high_code), own, gate, retain, zero, 0, owned, 0)
    out1, sums = combine(True, near, own, gate, retain, sums, owned, owned, chunk)
    out2, sums = combine(True, next_, own, gate, retain, sums, 2 * owned, owned, 2 * chunk)
    early = shared(sums)
    out = finish(order, early, [out0, out1, out2], 0, None, rows)
    out3, sums = combine(True, after(far_low, out), own, gate, retain, zero, 3 * owned, part, 0)
    out4, sums = combine(True, far_high, own, gate, retain, sums, 3 * owned + part, part, part * per)
    late = shared(sums)
    out = finish(order, late, [out3, out4], 3 * chunk, out, rows)
    return rows_unview(out, steps, layers)


def solution(mesh):
    return jax.shard_map(
        local,
        mesh=mesh,
        in_specs=(
            P("dp", None, "tensor", None, None),
            P(),
            P("dp"),
            P("dp", None, None, "tensor"),
            P("dp", None, None, "tensor"),
            P("dp", None, None, "tensor"),
            P("dp", None, None, "tensor"),
            P(None, "tensor"),
            P(None, "tensor"),
        ),
        out_specs=P("dp", None, None, "tensor"),
        check_vma=False,
    )
```

```python
import functools

import jax
import jax.numpy as jnp
from jax import lax
from jax.experimental import pallas as pl
from jax.experimental.pallas import tpu as pltpu
from jax.sharding import PartitionSpec as P

HEADS = 64
HEAD_DIM = 128
LANES = 128
ANY = pl.BlockSpec(memory_space=pl.ANY)
SMEM = pl.BlockSpec(memory_space=pltpu.SMEM)
VMEM = pl.BlockSpec(memory_space=pltpu.VMEM)
TOP = 32767.0
ROUND = 12582912.0
BIG = 54
FAR = 2


def params(mib):
    return pltpu.CompilerParams(vmem_limit_bytes=mib << 20)


def cost(flops, moved):
    return pl.CostEstimate(flops=flops, bytes_accessed=moved, transcendentals=0)


def rows_view(x):
    rows, steps, layers, columns = x.shape
    heads = columns // LANES
    x = x.reshape(rows, steps, layers, heads, LANES).transpose(0, 1, 3, 2, 4)
    return x.reshape(rows, steps * heads * layers, LANES)


def rows_unview(y, steps, layers):
    rows, lines, _ = y.shape
    heads = lines // (steps * layers)
    y = y.reshape(rows, steps, heads, layers, LANES).transpose(0, 1, 3, 2, 4)
    return y.reshape(rows, steps, layers, heads * LANES)


def iota(shape, axis):
    return lax.broadcasted_iota(jnp.int32, shape, axis)


def pack_rows(order_ref, first, prompts, q_ref, scratch, out_ref):
    lines = q_ref.shape[1]
    half = lines // 2
    total = out_ref.shape[1]
    samples = total // lines

    def body(p, carry):
        for c in range(samples):
            s = order_ref[0, first + p * samples + c]
            for j in range(2):
                block = q_ref[s, j * half : (j + 1) * half, :].astype(jnp.float32)
                scratch[p % 2, pl.ds(c * 2 + j, half, stride=2 * samples), :] = block
        out_ref[p] = scratch[p % 2].astype(jnp.bfloat16)
        return carry

    lax.fori_loop(0, prompts, body, 0, unroll=2)


def order_kernel(
    owned, quarter, chunks, place_ref, slot_hbm, prompt_hbm, q_hbm,
    order_ref, *rest,
):
    outs = rest[: len(chunks)]
    q_vmem, slot_ref, prompt_ref, line, scratch, sems = rest[len(chunks) :]
    small = [
        pltpu.make_async_copy(slot_hbm, slot_ref, sems.at[2]),
        pltpu.make_async_copy(prompt_hbm, prompt_ref, sems.at[3]),
    ]
    load = pltpu.make_async_copy(q_hbm, q_vmem, sems.at[0])
    for copy in small:
        copy.start()
    load.start()
    for copy in small:
        copy.wait()
    rows = prompt_ref.shape[1]
    count = slot_ref.shape[1]
    per = rows // (4 * owned)
    f32 = jnp.float32
    slot = slot_ref[...]
    owner = lax.div(lax.div(slot, owned), quarter)
    table = ((owner ^ place_ref[0, 0]) * owned + lax.rem(slot, owned)).astype(f32)
    down, across = iota((rows, rows), 0), iota((rows, rows), 1)
    prompt = jnp.broadcast_to(prompt_ref[...].astype(f32), (rows, rows))
    prompt = jnp.sum(jnp.where(down == across, prompt, 0.0), axis=1, keepdims=True)
    hit = prompt == iota((rows, count), 1).astype(f32)
    key = jnp.sum(jnp.where(hit, jnp.broadcast_to(table, (rows, count)), 0.0), axis=1, keepdims=True)
    key_all = jnp.broadcast_to(key, (rows, rows))
    key_row = jnp.sum(jnp.where(down == across, key_all, 0.0), axis=0, keepdims=True)
    same = (key_all == jnp.broadcast_to(key_row, (rows, rows))) & (across < down)
    rank = jnp.sum(jnp.where(same, 1.0, 0.0), axis=1, keepdims=True)
    spot = key * per + rank
    found = jnp.broadcast_to(spot, (rows, rows)) == across.astype(f32)
    line[...] = jnp.sum(jnp.where(found, down.astype(f32), 0.0), axis=0, keepdims=True).astype(jnp.int32)
    note = pltpu.make_async_copy(line, order_ref, sems.at[1])
    note.start()
    note.wait()
    load.wait()
    for chunk, out_ref in zip(chunks, outs):
        pack_rows(order_ref, chunk * owned * per, owned, q_vmem, scratch, out_ref)


def reach_kernel(coded, begin, prompts, q_ref, s_ref, out_ref, *scratch):
    heads = s_ref.shape[2]
    lines = q_ref.shape[1]
    lane = iota((8, LANES), 1)

    def products(p, h):
        a = q_ref[begin + p, h * 16 : (h + 1) * 16, :]
        w = jnp.concatenate([s_ref[begin + p, 0, h], s_ref[begin + p, 1, h]], axis=1)
        y = jnp.dot(a, w, preferred_element_type=jnp.float32)
        return y[:8, :LANES], y[8:, LANES:]

    def plain(p, carry):
        for h in range(heads):
            for l, r in enumerate(products(p, h)):
                at = h * 16 + l * 8
                out_ref[p, at : at + 8, :] = r
        return carry

    def code(t, carry):
        power = scratch[0]
        base = t * 2 * heads
        mine = (lane >= base) & (lane < base + 2 * heads)
        for slot in range(2):
            p = t * 2 + slot
            exponents = jnp.zeros((8, LANES), jnp.float32)
            for h in range(heads):
                pair = []
                for l, r in enumerate(products(p, h)):
                    top = jnp.max(jnp.abs(r), axis=1, keepdims=True)
                    e = jnp.ceil(jnp.log2(jnp.maximum(top, 1e-32)) + 1e-4)
                    exponents = jnp.where(lane == h * 2 + l, e, exponents)
                    pair.append((r * (jnp.exp2(15.0 - e) * (TOP / 32768.0)) + ROUND) - ROUND)
                pair = jnp.concatenate(pair, axis=0).astype(jnp.int32).astype(jnp.int16)
                out_ref[pl.ds(pl.multiple_of(p * lines + h * 16, 16), 16), :] = pair
            at = slice(slot * 8, slot * 8 + 8)
            power[at, :] = jnp.where(mine, pltpu.roll(exponents, base, 1), power[at, :])
        return carry

    if not coded:
        lax.fori_loop(0, prompts, plain, 0)
        return
    scratch[0][...] = jnp.zeros_like(scratch[0])
    lax.fori_loop(0, prompts // 2, code, 0, unroll=2)
    tail = prompts * lines
    out_ref[tail : tail + 16, :] = scratch[0][...].astype(jnp.int32).astype(jnp.int16)


def reach(query, states, begin, prompts, coded):
    _, lines, _ = query.shape
    _, layers, heads, _, _ = states.shape
    if coded:
        shape = jax.ShapeDtypeStruct((prompts * lines + 16, LANES), jnp.int16)
        scratch = [pltpu.VMEM((16, LANES), jnp.float32)]
    else:
        shape = jax.ShapeDtypeStruct((prompts, lines, LANES), jnp.float32)
        scratch = []
    return pl.pallas_call(
        functools.partial(reach_kernel, coded, begin, prompts),
        in_specs=[VMEM, VMEM],
        out_specs=VMEM,
        out_shape=shape,
        scratch_shapes=scratch,
        compiler_params=params(16),
        cost_estimate=cost(prompts * lines * LANES * LANES * 4, prompts * layers * heads * LANES * LANES * 2),
        name="reach",
    )(query, states)


def retained(decay_ref):
    layers, heads = decay_ref.shape
    line, head = iota((layers * heads, heads), 0), iota((layers * heads, heads), 1)
    rate = jnp.broadcast_to(decay_ref[0:1, :], (layers * heads, heads))
    other = jnp.broadcast_to(decay_ref[1:2, :], (layers * heads, heads))
    rate = jnp.where(line % 2 == 0, rate, other)
    rate = jnp.sum(jnp.where(line // 2 == head, rate, 0.0), axis=1, keepdims=True)
    return jnp.broadcast_to(jnp.exp(-rate), (layers * heads, LANES))


def row_terms(q_ref, k_ref, v_ref, g_ref, retain_ref, gain_ref, s):
    half = q_ref.shape[1] // 2
    f32 = jnp.float32
    one, two = slice(0, half), slice(half, 2 * half)
    retain, gain = retain_ref[...], gain_ref[...]
    q1, q2 = q_ref[s, one, :].astype(f32), q_ref[s, two, :].astype(f32)
    k1, k2 = k_ref[s, one, :].astype(f32), k_ref[s, two, :].astype(f32)
    v1, v2 = v_ref[s, one, :].astype(f32), v_ref[s, two, :].astype(f32)
    first_first = jnp.sum(q1 * k1, axis=1, keepdims=True)
    second_first = jnp.sum(q2 * k1, axis=1, keepdims=True)
    second_second = jnp.sum(q2 * k2, axis=1, keepdims=True)
    own = first_first * v1, retain * second_first * v1 + second_second * v2
    return own, [gain * jax.nn.sigmoid(g_ref[s, at, :].astype(f32)) for at in (one, two)]


def pack_kernel(
    per, owned, first, order_ref, decay_ref, gain_ref, q_hbm, k_hbm, v_hbm, g_hbm,
    far_ref, mine_ref, own_hbm, gate_hbm,
    q_ref, k_ref, v_ref, g_ref, own_ref, gate_ref, retain_ref, scratch, sems,
):
    half = q_ref.shape[1] // 2
    pairs = ((q_hbm, q_ref), (k_hbm, k_ref), (v_hbm, v_ref), (g_hbm, g_ref))
    loads = [pltpu.make_async_copy(a, b, sems.at[i]) for i, (a, b) in enumerate(pairs)]
    for copy in loads:
        copy.start()
    retain_ref[...] = retained(decay_ref)
    loads[0].wait()
    pack_rows(order_ref, 3 * owned * per, owned, q_ref, scratch, far_ref)
    pack_rows(order_ref, 0, owned, q_ref, scratch, mine_ref)
    for copy in loads[1:]:
        copy.wait()

    def body(i, carry):
        s = order_ref[0, first + i]
        own, gate = row_terms(q_ref, k_ref, v_ref, g_ref, retain_ref, gain_ref, s)
        for j in range(2):
            at = slice(j * half, (j + 1) * half)
            own_ref[i, at, :] = own[j]
            gate_ref[i, at, :] = gate[j]
        return carry

    rows = own_ref.shape[0]
    stores = []
    for n in range(4):
        at = pl.ds(n * (rows // 4), rows // 4)
        lax.fori_loop(n * (rows // 4), (n + 1) * (rows // 4), body, 0, unroll=2)
        for m, (a, b) in enumerate(((own_ref, own_hbm), (gate_ref, gate_hbm))):
            stores.append(pltpu.make_async_copy(a.at[at], b.at[at], sems.at[4 + 2 * n + m]))
            stores[-1].start()
    for copy in stores:
        copy.wait()


def combine_kernel(parts, inline, order_ref, decay_ref, sum_in, *refs):
    given, refs = refs[: 5 if inline else 2], refs[5 if inline else 2 :]
    product_refs, refs = refs[: len(parts)], refs[len(parts) :]
    out_refs, (sum_ref, retain_ref, unit_ref, exact) = refs[: len(parts)], refs[len(parts) :]
    half, total = retain_ref.shape[0], exact.shape[1]
    lane = iota((8, LANES), 1)
    retain_ref[...] = retained(decay_ref)
    zero = jnp.zeros((8, LANES), jnp.float32)
    totals = (zero, zero)
    for (coded, first, prompts, place), product_ref, out_ref in zip(parts, product_refs, out_refs):
        samples = out_ref.shape[0] // prompts
        if coded:
            power = product_ref[prompts * total : prompts * total + 16, :]
            unit_ref[...] = jnp.exp2(power.astype(jnp.int32).astype(jnp.float32) - 15.0) * (32768.0 / TOP)

        def body(t, totals, coded=coded, first=first, place=place, product_ref=product_ref, out_ref=out_ref, samples=samples):
            totals = list(totals)
            for slot in range(2):
                p = t * 2 + slot
                if coded:
                    unit = unit_ref[slot * 8 : slot * 8 + 8, :]
                    unit = pltpu.roll(unit, lax.rem(LANES - t * half, LANES), 1)
                    for h in range(half // 2):
                        code = product_ref[pl.ds(pl.multiple_of(p * total + h * 16, 16), 16), :]
                        code = code.astype(jnp.int32).astype(jnp.float32)
                        for l in range(2):
                            at = h * 16 + l * 8
                            u = jnp.broadcast_to(unit[:, h * 2 + l : h * 2 + l + 1], (8, LANES))
                            exact[slot, at : at + 8, :] = code[l * 8 : l * 8 + 8] * u
                    reached = exact.at[slot]
                else:
                    reached = product_ref.at[p]
                retain = retain_ref[...]
                squared = retain * retain
                for c in range(samples):
                    i = p * samples + c
                    if inline:
                        own, gate = row_terms(*given[:4], retain_ref, given[4], order_ref[0, first + i])
                    for j in range(2):
                        at = slice(j * half, (j + 1) * half)
                        r = reached[pl.ds(c * 2 + j, half, stride=2 * samples), :]
                        mixed = (squared if j else retain) * r + (own[j] if inline else given[0][place + i, at, :])
                        out_ref[i, at, :] = mixed * (gate[j] if inline else given[1][place + i, at, :])
                        power = jnp.sum((mixed * mixed).reshape(half // 8, 8, LANES), axis=0)
                        power = jnp.sum(power, axis=1, keepdims=True)
                        totals[j] = jnp.where(lane == first + i, power, totals[j])
            return tuple(totals)

        totals = lax.fori_loop(0, prompts // 2, body, totals)
    for j, t in enumerate(totals):
        u = t + pltpu.roll(t, 4, 0)
        sum_ref[j * 8 : j * 8 + 8] = u + pltpu.roll(u, 2, 0) + sum_in[j * 8 : j * 8 + 8]


def combine(order, decay, sums, given, parts):
    lines = given[0].shape[1]
    products = [p[4] for p in parts]
    total = max(x.shape[1] if not p[0] else (x.shape[0] - 16) // p[2] for x, p in zip(products, parts))
    samples = total // lines
    outs = [jax.ShapeDtypeStruct((p[2] * samples, lines, LANES), jnp.float32) for p in parts]
    count = sum(p[2] for p in parts) * samples
    return pl.pallas_call(
        functools.partial(combine_kernel, tuple(p[:4] for p in parts), len(given) == 5),
        in_specs=[SMEM] + [VMEM] * (2 + len(given) + len(parts)),
        out_specs=[VMEM] * (len(parts) + 1),
        out_shape=[*outs, jax.ShapeDtypeStruct((16, LANES), jnp.float32)],
        scratch_shapes=[
            pltpu.VMEM((lines // 2, LANES), jnp.float32),
            pltpu.VMEM((16, LANES), jnp.float32),
            pltpu.VMEM((2, total, LANES), jnp.float32),
        ],
        compiler_params=params(16),
        cost_estimate=cost(0, count * lines * LANES * 14),
        name="combine",
    )(order, decay, sums, *given, *products)


def finish_kernel(features, first, splits, count, order_ref, *refs):
    tiles, refs = refs[:count], refs[count:]
    parts, (out_hbm, scratch, scale, sem) = refs[: len(splits)], refs[-4:]
    half = parts[0].shape[1] // 2
    total = sum(t[...] for t in tiles)
    scale[...] = lax.rsqrt(total / features + 1e-05)
    at = 0
    for part, rows in zip(parts, splits):

        def body(b, carry, part=part, at=at):
            turned = pltpu.roll(scale[...], lax.rem(2 * LANES - first - at - b * 8, LANES), 1)
            for i in range(8):
                row = b * 8 + i
                for j in range(2):
                    one = jnp.broadcast_to(turned[j * 8 : j * 8 + 8, i : i + 1], (8, LANES))
                    lines = part[row, j * half : (j + 1) * half, :].reshape(half // 8, 8, LANES)
                    scratch[at + row, j * half : (j + 1) * half, :] = (lines * one[None]).reshape(half, LANES)
                s = order_ref[0, first + at + row]
                pltpu.make_async_copy(scratch.at[at + row], out_hbm.at[s], sem).start()
            return carry

        lax.fori_loop(0, rows // 8, body, 0)
        at += rows
    pltpu.make_async_copy(scratch, out_hbm.at[pl.ds(0, at)], sem).wait()


def finish(order, tiles, parts, first, out, rows):
    splits = tuple(p.shape[0] for p in parts)
    lines = parts[0].shape[1]
    given = [order, *tiles, *parts] + ([] if out is None else [out])
    return pl.pallas_call(
        functools.partial(finish_kernel, HEADS * HEAD_DIM, first, splits, len(tiles)),
        in_specs=[SMEM] + [VMEM] * (len(tiles) + len(parts)) + ([] if out is None else [ANY]),
        out_specs=ANY,
        out_shape=jax.ShapeDtypeStruct((rows, lines, LANES), jnp.float32),
        scratch_shapes=[
            pltpu.VMEM((sum(splits), lines, LANES), jnp.float32),
            pltpu.VMEM((16, LANES), jnp.float32),
            pltpu.SemaphoreType.DMA,
        ],
        input_output_aliases={} if out is None else {len(given) - 1: 0},
        compiler_params=params(16),
        cost_estimate=cost(0, sum(splits) * lines * LANES * 8),
        name="finish",
    )(*given)


def local(
    prefill_states, prompt_slot, sample_prompt, queries, keys, values, gates, norm_gain, decay_rate
):
    group = lax.axis_index("dp")
    groups = lax.axis_size("dp")
    split = lax.axis_size("tensor")
    quarter = groups // 4
    owned = prefill_states.shape[0]
    rows, steps, layers, columns = queries.shape
    heads = columns // LANES
    per = rows // (4 * owned)
    lines = steps * layers * heads
    assert steps == 2 and layers == 2 and per * steps == 8 and rows <= LANES
    assert heads % 4 == 0 and heads * layers * owned <= 2 * LANES

    def swap(block, bits):
        far = [((i // quarter) ^ bits) * quarter + i % quarter for i in range(groups)]
        return lax.ppermute(block, "dp", [(f, i) for i, f in enumerate(far)])

    def shared(tile):
        if split not in (2, 4):
            return [lax.psum(tile, "tensor")]
        return [tile] + [
            lax.ppermute(tile, "tensor", [(i, i ^ k) for i in range(split)])
            for k in range(1, split)
        ]

    q, k, v, g = (rows_view(x) for x in (queries, keys, values, gates))
    gain = rows_view(norm_gain[None, None]).reshape(heads * layers, LANES)
    place = (group // quarter).astype(jnp.int32).reshape(1, 1)

    packed = jax.ShapeDtypeStruct((owned, per * lines, LANES), jnp.bfloat16)
    pack_scratch = pltpu.VMEM((2, per * lines, LANES), jnp.float32)
    order, near, next_ = pl.pallas_call(
        functools.partial(order_kernel, owned, quarter, (1, 2)),
        in_specs=[SMEM, ANY, ANY, ANY],
        out_specs=[SMEM, VMEM, VMEM],
        out_shape=[jax.ShapeDtypeStruct((1, rows), jnp.int32), packed, packed],
        scratch_shapes=[
            pltpu.VMEM(q.shape, q.dtype),
            pltpu.VMEM((1, prompt_slot.shape[0]), jnp.int32),
            pltpu.VMEM((1, rows), jnp.int32),
            pltpu.VMEM((1, rows), jnp.int32),
            pack_scratch,
            pltpu.SemaphoreType.DMA((4,)),
        ],
        compiler_params=params(60),
        cost_estimate=cost(0, 4 << 20),
        name="order",
    )(place, prompt_slot.reshape(1, -1), sample_prompt.reshape(1, -1), q)
    near, next_ = swap(near, 1), swap(next_, 2)
    chunk = owned * per
    ready = jax.ShapeDtypeStruct((chunk, lines, LANES), jnp.float32)
    far, mine, own, gate = pl.pallas_call(
        functools.partial(pack_kernel, per, owned, 3 * chunk),
        in_specs=[SMEM, VMEM, VMEM] + [ANY] * 4,
        out_specs=[VMEM, VMEM, ANY, ANY],
        out_shape=[packed, packed, ready, ready],
        scratch_shapes=[pltpu.VMEM(q.shape, q.dtype)] * 4
        + [pltpu.VMEM(ready.shape, jnp.float32)] * 2
        + [pltpu.VMEM(gain.shape, jnp.float32), pack_scratch, pltpu.SemaphoreType.DMA((12,))],
        compiler_params=params(BIG),
        cost_estimate=cost(0, 16 << 20),
        name="pack",
    )(order, decay_rate, gain, q, k, v, g)

    def after(value, *done):
        return lax.optimization_barrier((value, *done))[0]

    mine = reach(mine, prefill_states, 0, owned, False)
    far = swap(after(far, mine), 3)
    near_code = reach(after(near, mine), prefill_states, 0, owned, True)
    near = swap(near_code, 1)
    next_code = reach(after(next_, near_code), prefill_states, 0, owned, True)
    next_ = swap(next_code, 2)
    cuts = [owned // FAR * i for i in range(FAR + 1)]
    far_codes, code = [], next_code
    for begin, end in zip(cuts, cuts[1:]):
        code = reach(after(far, code), prefill_states, begin, end - begin, True)
        far_codes.append(swap(code, 3))

    zero = after(jnp.zeros((16, LANES), jnp.float32), code)
    sums, outs = zero, []
    for part in ((False, 0, owned, 0, mine), (True, chunk, owned, 0, near), (True, 2 * chunk, owned, 0, next_)):
        more, sums = combine(order, decay_rate, sums, (q, k, v, g, gain), [part])
        outs.append(more)
    early = shared(sums)
    sums, lates = zero, []
    for begin, end, x in zip(cuts, cuts[1:], far_codes):
        part = (True, 3 * chunk + begin * per, end - begin, begin * per, x)
        more, sums = combine(order, decay_rate, sums, (own, gate), [part])
        lates.append(more)
    late = shared(sums)
    out = finish(order, early, outs, 0, None, rows)
    out = finish(order, late, lates, 3 * chunk, out, rows)
    return rows_unview(out, steps, layers)


def solution(mesh):
    return jax.shard_map(
        local,
        mesh=mesh,
        in_specs=(
            P("dp", None, "tensor", None, None),
            P(),
            P("dp"),
            P("dp", None, None, "tensor"),
            P("dp", None, None, "tensor"),
            P("dp", None, None, "tensor"),
            P("dp", None, None, "tensor"),
            P(None, "tensor"),
            P(None, "tensor"),
        ),
        out_specs=P("dp", None, None, "tensor"),
        check_vma=False,
    )
```
